32 devices in a mesh: ia: 4 (over y, core), ja: 2 (over x), ka: 4 (over z).
Axes of the slice: x: 2, y: 2, z: 4, core: 2. Of those that a mesh axis runs over, the one named last changes fastest.
Arguments:
- block_coords: int32 [4, 2, 4, 4, 3], P('ia', 'ja', 'ka'), may hold values from 0 to 3, as said below
- live_blocks: int32 [4, 2, 4], P('ia', 'ja', 'ka'), may hold values from 1 to 4, as said below
- counts: int32 [4, 2, 4, 4, 64, 4096], P('ia', 'ja', 'ka'), may hold values from 0 to 7
- factor_a: float32 [1024, 256], P(('ia', 'ja', 'ka')), may hold values from 0.3 to 9.6
- factor_b: float32 [512, 256], P(('ja', 'ka')), may hold values from 0.05 to 8
- factor_c: float32 [1024, 256], P('ka', 'ia'), may hold values from 0.05 to 8
Outputs:
- factor_new: float32 [1024, 256], P(('ia', 'ja', 'ka'))
The draws below stay inside these ranges and needn't reach their ends.
Inputs may be any that keep to these rules, and one draw needn't show every extreme that they name: `block_coords`: a device's slots name distinct blocks; slot 0 is always live, and every mode-1 block of the slab has a live block on some device. `live_blocks`: on some device all 4 slots are live.
All inputs are finite; a program needn't handle non-finite values.
Results may differ from the reference program's by a relative error of at most 0.00061.
Values may be sent and summed in bfloat16 or wider, within the bound.
A program may use at most 64 MiB of HBM per device.

```python
import math
import jax
import jax.numpy as jnp
from jax import lax

R = 256
BS = 64
RB1 = 4
RB2 = 4
RB3 = 4
SLOTS = 4
ROWS_I = 1024
ROWS_J = 512
ROWS_K = 1024
N_IA = 4
N_JA = 2
N_KA = 4


def draw_block_coords(key, part):
    total = N_IA * N_JA * N_KA
    many = RB1 * RB2 * RB3

    def single(index):
        sub = jax.random.fold_in(jax.random.fold_in(key, 11), index)
        first_key, other_key = jax.random.split(sub)
        group = index % (N_JA * N_KA) % RB1
        chosen = group * (RB2 * RB3) + jax.random.randint(first_key, (), 0, RB2 * RB3)
        positions = jnp.arange(many, dtype=jnp.int32)
        scores = jax.random.randint(other_key, (many,), 0, 2 ** 16) * many + positions
        scores = jnp.where(positions == chosen, 2 ** 30, scores)
        order = jnp.argsort(scores, stable=True).astype(jnp.int32)
        picked = jnp.concatenate([chosen[None].astype(jnp.int32), order[:SLOTS - 1]])
        return jnp.stack([picked // (RB2 * RB3), picked // RB3 % RB2, picked % RB3], axis=-1)
    result = jax.vmap(single)(jnp.arange(total, dtype=jnp.int32))
    return result.reshape(N_IA, N_JA, N_KA, SLOTS, 3).astype(jnp.int32)


def draw_live_blocks(key, part):
    total = N_IA * N_JA * N_KA
    key_base, key_busy, key_forced = jax.random.split(jax.random.fold_in(key, 23), 3)
    base = jax.random.randint(key_base, (total,), 1, max(2, SLOTS // 2 + 1))
    busy = jax.random.randint(key_busy, (total,), 0, 8) == 0
    forced = jax.random.randint(key_forced, (), 0, total)
    result = jnp.where(busy | (jnp.arange(total) == forced), SLOTS, base)
    return result.reshape(N_IA, N_JA, N_KA).astype(jnp.int32)


def topic_factor(key, seed_offset, row_count, lowest, highest, factor_boost):
    folded = jax.random.fold_in(key, seed_offset)
    key_level, key_marked = jax.random.split(folded)
    base_level = jnp.exp(jax.random.uniform(key_level, (row_count, R), jnp.float32, math.log(lowest), math.log(highest)))
    marked = jax.random.randint(key_marked, (row_count, R), 0, 32) == 0
    return jnp.where(marked, base_level * factor_boost, base_level).astype(jnp.float32)


def draw_factor_a(key, part):
    return topic_factor(key, 31, ROWS_I, 0.3, 1.2, 8.0)


def draw_factor_b(key, part):
    factor_boost = 30.0
    return topic_factor(key, 37, ROWS_J, 0.05, 0.2, factor_boost)


def draw_factor_c(key, part):
    factor_boost = 30.0
    return topic_factor(key, 41, ROWS_K, 0.05, 0.2, factor_boost)


def plant(values, own_key, low, top_value):
    index_at = [jax.random.randint(jax.random.fold_in(own_key, axis), (), 0, length) for axis, length in enumerate(values.shape)]
    widest = values.shape.index(max(values.shape))
    neighbour = index_at[:widest] + [(index_at[widest] + 1) % values.shape[widest]] + index_at[widest + 1:]
    return values.at[tuple(index_at)].set(low).at[tuple(neighbour)].set(top_value)


def setup_inputs(seed: int = 0) -> dict:
    streams_of = jax.random.split(jax.random.key(seed), 7)
    return {
        "block_coords": draw_block_coords(jax.random.fold_in(streams_of[6], 71), 0),
        "live_blocks": draw_live_blocks(jax.random.fold_in(streams_of[6], 71), 0),
        "counts": plant(jax.random.randint(streams_of[2], (N_IA, N_JA, N_KA, SLOTS, BS, BS * BS), 0, 8), jax.random.fold_in(streams_of[2], 1), 0, 7).astype(jnp.int32),
        "factor_a": draw_factor_a(jax.random.fold_in(streams_of[6], 71), 0),
        "factor_b": draw_factor_b(jax.random.fold_in(streams_of[6], 71), 0),
        "factor_c": draw_factor_c(jax.random.fold_in(streams_of[6], 71), 0),
    }


def reference(block_coords, live_blocks, counts, factor_a, factor_b, factor_c):
    devices_all = N_IA * N_JA * N_KA
    total = devices_all * SLOTS
    flat_coords = block_coords.reshape(total, 3)
    entry = jnp.arange(total, dtype=jnp.int32)
    device = entry // SLOTS
    slot = entry % SLOTS
    a_index = device // (N_JA * N_KA)
    b_index = (device // N_KA) % N_JA
    c_index = device % N_KA
    weight = (slot < live_blocks.reshape(devices_all)[device]).astype(jnp.float32)
    block_i = (a_index * RB1 + flat_coords[:, 0]).astype(jnp.int32)
    block_j = (b_index * RB2 + flat_coords[:, 1]).astype(jnp.int32)
    block_k = (c_index * RB3 + flat_coords[:, 2]).astype(jnp.int32)
    flat_counts = counts.reshape(total, BS, BS * BS)
    sums_b = factor_b.reshape(N_JA * RB2, BS, R).sum(axis=1)
    sums_c = factor_c.reshape(N_KA * RB3, BS, R).sum(axis=1)
    masses = sums_b[block_j] * sums_c[block_k] * weight[:, None]
    mass = jax.ops.segment_sum(masses, block_i, num_segments=N_IA * RB1)
    mass_rows = jnp.repeat(mass, BS, axis=0)

    def accumulate(factor):
        factor_low = factor.astype(jnp.bfloat16)

        def step(phi, item):
            gi, gj, gk, w, block_counts = item
            rows_b = lax.dynamic_slice_in_dim(factor_b, gj * BS, BS, 0)
            rows_c = lax.dynamic_slice_in_dim(factor_c, gk * BS, BS, 0)
            panel = (rows_b[:, None, :] * rows_c[None, :, :]).reshape(BS * BS, R).astype(jnp.bfloat16)
            block_a = lax.dynamic_slice_in_dim(factor_low, gi * BS, BS, 0)
            model = lax.dot_general(block_a, panel, (((1,), (1,)), ((), ())), preferred_element_type=jnp.float32)
            ratio = (block_counts.astype(jnp.float32) / model).astype(jnp.bfloat16)
            part = jnp.dot(ratio, panel, preferred_element_type=jnp.float32) * w
            old = lax.dynamic_slice_in_dim(phi, gi * BS, BS, 0)
            return lax.dynamic_update_slice_in_dim(phi, old + part, gi * BS, 0), None

        start = jnp.zeros((N_IA * RB1 * BS, R), jnp.float32)
        phi, _ = lax.scan(step, start, (block_i, block_j, block_k, weight, flat_counts))
        return phi

    first = factor_a * accumulate(factor_a) / mass_rows
    return first * accumulate(first) / mass_rows
```

```python
import functools

import jax
import jax.numpy as jnp
from jax import lax
from jax.experimental import pallas as pl
from jax.experimental.pallas import tpu as pltpu
from jax.sharding import PartitionSpec as P

RB1 = 4
RB2 = 4
RB3 = 4
MESH = pl.DeviceIdType.MESH


def loop(count, body):
    if count <= 8:
        for d in range(1, count):
            body(d)
    else:

        def step(d, carry):
            body(d)
            return carry

        lax.fori_loop(1, count, step, 0)


def kernel(
    n_ia, n_ja, n_ka, bs,
    coords, live, counts, fa, fb, fc, out,
    cnt, bg, cg, cfull, aown, alow, al, afull, panel, phi, ps, pr, ms, mr,
    local_sem, b_send, b_recv, c_send, c_recv, g_send, g_recv,
):
    n = n_ja * n_ka
    ia, ja, ka = lax.axis_index("ia"), lax.axis_index("ja"), lax.axis_index("ka")
    me = ja * n_ka + ka
    slots = cnt.shape[0]
    owned, rank = aown.shape
    rb = fb.shape[0]
    wc = fc.shape[0]

    def group(d):
        t = lax.rem(me + d, n)
        return {"ja": lax.div(t, n_ka), "ka": lax.rem(t, n_ka)}

    def source(d):
        return lax.rem(me + n - d, n)

    load_a = pltpu.make_async_copy(fa, aown, local_sem.at[0])
    own_rows = pl.ds(pl.multiple_of(ka * rb, rb), rb)
    load_b = pltpu.make_async_copy(fb, bg.at[own_rows], local_sem.at[1])
    own_ranks = pl.ds(pl.multiple_of(ia * wc, wc), wc)
    load_c = pltpu.make_async_copy(fc, cg.at[own_ranks], local_sem.at[2])
    load_n = pltpu.make_async_copy(counts, cnt, local_sem.at[3])
    load_a.start()
    load_b.start()
    load_c.start()
    load_n.start()

    barrier = pltpu.get_barrier_semaphore()
    loop(n, lambda d: pl.semaphore_signal(barrier, inc=1, device_id=group(d), device_id_type=MESH))
    loop(
        n_ia,
        lambda d: pl.semaphore_signal(
            barrier, inc=1, device_id={"ia": lax.rem(ia + d, n_ia)}, device_id_type=MESH
        ),
    )
    load_a.wait()
    alow[0] = aown[...].astype(jnp.bfloat16)
    pl.semaphore_wait(barrier, n + n_ia - 2)

    def b_copy(d, whose):
        rows = pl.ds(pl.multiple_of(whose * rb, rb), rb)
        return pltpu.make_async_remote_copy(
            src_ref=fb, dst_ref=bg.at[rows], send_sem=b_send.at[d], recv_sem=b_recv.at[d],
            device_id={"ka": lax.rem(ka + d, n_ka)}, device_id_type=MESH,
        )

    def c_copy(d, whose):
        ranks = pl.ds(pl.multiple_of(whose * wc, wc), wc)
        return pltpu.make_async_remote_copy(
            src_ref=fc, dst_ref=cg.at[ranks], send_sem=c_send.at[d], recv_sem=c_recv.at[d],
            device_id={"ia": lax.rem(ia + d, n_ia)}, device_id_type=MESH,
        )

    def a_copy(turn, d, whose):
        return pltpu.make_async_remote_copy(
            src_ref=alow.at[turn], dst_ref=al.at[turn, whose],
            send_sem=g_send.at[turn, d], recv_sem=g_recv.at[turn, d],
            device_id=group(d), device_id_type=MESH,
        )

    def phi_copy(turn, d, whose):
        return pltpu.make_async_remote_copy(
            src_ref=ps.at[lax.rem(me + d, n)], dst_ref=pr.at[turn, whose],
            send_sem=g_send.at[2 + turn, d], recv_sem=g_recv.at[2 + turn, d],
            device_id=group(d), device_id_type=MESH,
        )

    def mass_copy(d, whose):
        block = lax.div(lax.rem(me + d, n) * owned, bs)
        return pltpu.make_async_remote_copy(
            src_ref=ms.at[block], dst_ref=mr.at[whose],
            send_sem=g_send.at[4, d], recv_sem=g_recv.at[4, d],
            device_id=group(d), device_id_type=MESH,
        )

    loop(n_ka, lambda d: b_copy(d, ka).start())
    loop(n_ia, lambda d: c_copy(d, ia).start())
    loop(n, lambda d: a_copy(0, d, me).start())

    phi[...] = jnp.zeros_like(phi)
    ms[...] = jnp.zeros_like(ms)
    load_b.wait()
    load_c.wait()
    loop(n_ia, lambda d: c_copy(d, lax.rem(ia + n_ia - d, n_ia)).wait_recv())
    cfull[...] = cg[...].T
    loop(n_ka, lambda d: b_copy(d, lax.rem(ka + n_ka - d, n_ka)).wait_recv())

    def is_block(index, q):
        return jnp.full((bs, rank), index, jnp.int32) == q

    def live_weight(s):
        return jnp.minimum(jnp.maximum(live[0] - s, 0), 1).astype(jnp.float32)

    def piece(ref, index):
        found = ref[:bs]
        for q in range(1, ref.shape[0] // bs):
            found = jnp.where(is_block(index, q), ref[q * bs:(q + 1) * bs], found)
        return found

    def build(s, carry):
        rows_b = piece(bg, coords[s, 1])
        rows_c = piece(cfull, coords[s, 2])
        mass = jnp.sum(rows_b, axis=0, keepdims=True) * jnp.sum(rows_c, axis=0, keepdims=True)
        mass = mass * live_weight(s)
        for q in range(RB1):
            ms[q] += jnp.where(is_block(coords[s, 0], q)[:1], mass, 0.0)
        for j in range(bs):
            panel[s, j * bs:(j + 1) * bs] = (rows_b[j:j + 1] * rows_c).astype(jnp.bfloat16)
        return carry

    lax.fori_loop(0, slots, build, 0)
    loop(n, lambda d: mass_copy(d, me).start())
    mr[me] = ms[lax.div(me * owned, bs)]
    load_n.wait()

    def gathered(turn):
        al[turn, me] = alow[turn]
        loop(n, lambda d: a_copy(turn, d, source(d)).wait_recv())
        for p in range(n):
            afull[p * owned:(p + 1) * owned] = al[turn, p].astype(jnp.float32)

    step_columns = min(1024, bs * bs)

    def accumulate(s, carry):
        block_a = piece(afull, coords[s, 0]).astype(jnp.bfloat16)
        part = jnp.zeros((bs, rank), jnp.float32)
        for first in range(0, bs * bs, step_columns):
            rows = panel[s, first:first + step_columns]
            model = lax.dot_general(
                block_a, rows, (((1,), (1,)), ((), ())), preferred_element_type=jnp.float32
            )
            here = cnt[s, :, first:first + step_columns].astype(jnp.float32)
            ratio = (here / model).astype(jnp.bfloat16)
            part += jnp.dot(ratio, rows, preferred_element_type=jnp.float32)
        part = part * live_weight(s)
        for q in range(RB1):
            phi[q * bs:(q + 1) * bs] += jnp.where(is_block(coords[s, 0], q), part, 0.0)
        return carry

    def scattered(turn):
        for p in range(n):
            ps[p] = phi[p * owned:(p + 1) * owned]
        loop(n, lambda d: phi_copy(turn, d, me).start())
        pr[turn, me] = ps[me]
        loop(n, lambda d: phi_copy(turn, d, source(d)).wait_recv())
        total = pr[turn, 0]
        for p in range(1, n):
            total += pr[turn, p]
        return total

    gathered(0)
    lax.fori_loop(0, slots, accumulate, 0)
    total = scattered(0)
    loop(n, lambda d: mass_copy(d, source(d)).wait_recv())
    mass = mr[0]
    for p in range(1, n):
        mass += mr[p]
    updated = aown[...] * total / mass
    alow[1] = updated.astype(jnp.bfloat16)
    loop(n, lambda d: a_copy(1, d, me).start())
    phi[...] = jnp.zeros_like(phi)
    loop(n, lambda d: phi_copy(0, d, me).wait_send())
    aown[...] = updated
    gathered(1)
    lax.fori_loop(0, slots, accumulate, 0)
    total = scattered(1)
    out[...] = aown[...] * total / mass

    loop(n_ka, lambda d: b_copy(d, ka).wait_send())
    loop(n_ia, lambda d: c_copy(d, ia).wait_send())
    loop(n, lambda d: a_copy(0, d, me).wait_send())
    loop(n, lambda d: a_copy(1, d, me).wait_send())
    loop(n, lambda d: mass_copy(d, me).wait_send())
    loop(n, lambda d: phi_copy(1, d, me).wait_send())


def local(n_ia, n_ja, n_ka, block_coords, live_blocks, counts, factor_a, factor_b, factor_c):
    slots = block_coords.shape[-2]
    bs, cells = counts.shape[-2:]
    owned, rank = factor_a.shape
    rb = factor_b.shape[0]
    rc, wc = factor_c.shape
    n = n_ja * n_ka
    f32, bf16 = jnp.float32, jnp.bfloat16
    smem = pl.BlockSpec(memory_space=pltpu.SMEM)
    hbm = pl.BlockSpec(memory_space=pl.ANY)
    dma = pltpu.SemaphoreType.DMA
    return pl.pallas_call(
        functools.partial(kernel, n_ia, n_ja, n_ka, bs),
        out_shape=jax.ShapeDtypeStruct((owned, rank), f32),
        in_specs=[smem, smem, hbm, hbm, hbm, hbm],
        out_specs=pl.BlockSpec(memory_space=pltpu.VMEM),
        scratch_shapes=[
            pltpu.VMEM((slots, bs, cells), jnp.int32),
            pltpu.VMEM((n_ka * rb, rank), f32),
            pltpu.VMEM((n_ia * wc, rc), f32),
            pltpu.VMEM((rc, rank), f32),
            pltpu.VMEM((owned, rank), f32),
            pltpu.VMEM((2, owned, rank), bf16),
            pltpu.VMEM((2, n, owned, rank), bf16),
            pltpu.VMEM((RB1 * bs, rank), f32),
            pltpu.VMEM((slots, cells, rank), bf16),
            pltpu.VMEM((RB1 * bs, rank), f32),
            pltpu.VMEM((n, owned, rank), f32),
            pltpu.VMEM((2, n, owned, rank), f32),
            pltpu.VMEM((RB1, 1, rank), f32),
            pltpu.VMEM((n, 1, rank), f32),
            dma((4,)),
            dma((n_ka,)),
            dma((n_ka,)),
            dma((n_ia,)),
            dma((n_ia,)),
            dma((5, n)),
            dma((5, n)),
        ],
        compiler_params=pltpu.CompilerParams(
            collective_id=0, has_side_effects=True, vmem_limit_bytes=56 * 1024 * 1024
        ),
    )(
        block_coords.reshape(slots, 3), live_blocks.reshape(1),
        counts.reshape(slots, bs, cells), factor_a, factor_b, factor_c.T,
    )


def solution(mesh):
    placed = (
        P("ia", "ja", "ka", None, None),
        P("ia", "ja", "ka"),
        P("ia", "ja", "ka", None, None, None),
        P(("ia", "ja", "ka"), None),
        P(("ja", "ka"), None),
        P("ka", "ia"),
    )
    body = functools.partial(local, mesh.shape["ia"], mesh.shape["ja"], mesh.shape["ka"])
    return jax.shard_map(
        body, mesh=mesh, in_specs=placed, out_specs=P(("ia", "ja", "ka"), None), check_vma=False
    )
```

```python
import functools

import jax
import jax.numpy as jnp
from jax import lax
from jax.experimental import pallas as pl
from jax.experimental.pallas import tpu as pltpu
from jax.sharding import PartitionSpec as P

RB1 = 4
RB2 = 4
RB3 = 4
MESH = pl.DeviceIdType.MESH


def loop(count, body):
    if count <= 8:
        for d in range(1, count):
            body(d)
    else:

        def step(d, carry):
            body(d)
            return carry

        lax.fori_loop(1, count, step, 0)


def kernel(
    n_ia, n_ja, n_ka, bs,
    coords, live, counts, fa, fb, fc, out,
    cnt, bg, cg, cfull, aown, alow, al, afull, panel, phi, ps, pr, ms, mr,
    local_sem, b_send, b_recv, c_send, c_recv, g_send, g_recv,
):
    n = n_ja * n_ka
    ia, ja, ka = lax.axis_index("ia"), lax.axis_index("ja"), lax.axis_index("ka")
    me = ja * n_ka + ka
    slots = cnt.shape[0]
    owned, rank = aown.shape
    rb = fb.shape[0]
    wc = fc.shape[0]

    def group(d):
        t = lax.rem(me + d, n)
        return {"ja": lax.div(t, n_ka), "ka": lax.rem(t, n_ka)}

    def source(d):
        return lax.rem(me + n - d, n)

    load_a = pltpu.make_async_copy(fa, aown, local_sem.at[0])
    own_rows = pl.ds(pl.multiple_of(ka * rb, rb), rb)
    load_b = pltpu.make_async_copy(fb, bg.at[own_rows], local_sem.at[1])
    own_ranks = pl.ds(pl.multiple_of(ia * wc, wc), wc)
    load_c = pltpu.make_async_copy(fc, cg.at[own_ranks], local_sem.at[2])
    load_n = pltpu.make_async_copy(counts, cnt, local_sem.at[3])
    load_a.start()
    load_b.start()
    load_c.start()
    load_n.start()

    barrier = pltpu.get_barrier_semaphore()
    for axis, here, count in (("ka", ka, n_ka), ("ja", ja, n_ja), ("ia", ia, n_ia)):
        loop(
            count,
            lambda d: pl.semaphore_signal(
                barrier, inc=1, device_id={axis: lax.rem(here + d, count)}, device_id_type=MESH
            ),
        )
    load_a.wait()
    alow[0] = aown[...].astype(jnp.bfloat16)
    pl.semaphore_wait(barrier, n_ka + n_ja + n_ia - 3)

    halves = 2 if n_ia % 2 == 0 and rb % 16 == 0 else 1
    hb = rb // halves
    part = lax.rem(ia, halves)
    partner = ia + 1 - 2 * part

    def b_rows(whose, half):
        return bg.at[pl.ds(pl.multiple_of(whose * rb + half * hb, hb), hb)]

    def b_copy(d, whose):
        return pltpu.make_async_remote_copy(
            src_ref=fb.at[pl.ds(pl.multiple_of(part * hb, hb), hb)], dst_ref=b_rows(whose, part),
            send_sem=b_send.at[0, d], recv_sem=b_recv.at[0, d],
            device_id={"ka": lax.rem(ka + d, n_ka)}, device_id_type=MESH,
        )

    def b_hand(d, half):
        rows = b_rows(lax.rem(ka + n_ka - d, n_ka), half)
        return pltpu.make_async_remote_copy(
            src_ref=rows, dst_ref=rows, send_sem=b_send.at[1, d], recv_sem=b_recv.at[1, d],
            device_id={"ia": partner}, device_id_type=MESH,
        )

    def c_copy(d, whose):
        ranks = pl.ds(pl.multiple_of(whose * wc, wc), wc)
        return pltpu.make_async_remote_copy(
            src_ref=fc, dst_ref=cg.at[ranks], send_sem=c_send.at[d], recv_sem=c_recv.at[d],
            device_id={"ia": lax.rem(ia + d, n_ia)}, device_id_type=MESH,
        )

    def a_copy(d, whose):
        return pltpu.make_async_remote_copy(
            src_ref=alow.at[1], dst_ref=al.at[1, whose],
            send_sem=g_send.at[1, d], recv_sem=g_recv.at[1, d],
            device_id=group(d), device_id_type=MESH,
        )

    def a_across(d, whose):
        return pltpu.make_async_remote_copy(
            src_ref=alow.at[0], dst_ref=al.at[0, whose * n_ka + ka],
            send_sem=g_send.at[0, d * n_ka], recv_sem=g_recv.at[0, d * n_ka],
            device_id={"ja": lax.rem(ja + d, n_ja)}, device_id_type=MESH,
        )

    def a_along(e, d, whose):
        other = lax.rem(ja + n_ja - e, n_ja) * n_ka
        return pltpu.make_async_remote_copy(
            src_ref=alow.at[0] if isinstance(e, int) and e == 0 else al.at[0, other + ka],
            dst_ref=al.at[0, other + whose],
            send_sem=g_send.at[0, e * n_ka + d], recv_sem=g_recv.at[0, e * n_ka + d],
            device_id={"ka": lax.rem(ka + d, n_ka)}, device_id_type=MESH,
        )

    def phi_copy(turn, d, whose):
        return pltpu.make_async_remote_copy(
            src_ref=ps.at[lax.rem(me + d, n)], dst_ref=pr.at[turn, whose],
            send_sem=g_send.at[2 + turn, d], recv_sem=g_recv.at[2 + turn, d],
            device_id=group(d), device_id_type=MESH,
        )

    def mass_copy(d, whose):
        block = lax.div(lax.rem(me + d, n) * owned, bs)
        return pltpu.make_async_remote_copy(
            src_ref=ms.at[block], dst_ref=mr.at[whose],
            send_sem=g_send.at[4, d], recv_sem=g_recv.at[4, d],
            device_id=group(d), device_id_type=MESH,
        )

    loop(n_ka, lambda d: b_copy(d, ka).start())
    loop(n_ia, lambda d: c_copy(d, ia).start())
    loop(n_ja, lambda d: a_across(d, ja).start())
    loop(n_ka, lambda d: a_along(0, d, ka).start())
    al[0, me] = alow[0]

    phi[...] = jnp.zeros_like(phi)
    ms[...] = jnp.zeros_like(ms)
    load_b.wait()
    load_c.wait()


    def across(e):
        a_across(e, lax.rem(ja + n_ja - e, n_ja)).wait_recv()
        loop(n_ka, lambda d: a_along(e, d, ka).start())

    loop(n_ja, across)

    def hand_on(d):
        b_copy(d, lax.rem(ka + n_ka - d, n_ka)).wait_recv()
        if halves == 2:
            b_hand(d, part).start()

    loop(n_ka, hand_on)
    loop(n_ia, lambda d: c_copy(d, lax.rem(ia + n_ia - d, n_ia)).wait_recv())
    cfull[...] = cg[...].T
    if halves == 2:
        loop(n_ka, lambda d: b_hand(d, 1 - part).wait_recv())

    def is_block(index, q):
        return jnp.full((bs, rank), index, jnp.int32) == q

    def live_weight(s):
        return jnp.minimum(jnp.maximum(live[0] - s, 0), 1).astype(jnp.float32)

    def piece(ref, index):
        found = ref[:bs]
        for q in range(1, ref.shape[0] // bs):
            found = jnp.where(is_block(index, q), ref[q * bs:(q + 1) * bs], found)
        return found

    def build(s, carry):
        rows_b = piece(bg, coords[1, 0, s])
        rows_c = piece(cfull, coords[2, 0, s])
        mass = jnp.sum(rows_b, axis=0, keepdims=True) * jnp.sum(rows_c, axis=0, keepdims=True)
        mass = mass * live_weight(s)
        for q in range(RB1):
            ms[q] += jnp.where(is_block(coords[0, 0, s], q)[:1], mass, 0.0)
        return carry

    lax.fori_loop(0, slots, build, 0)
    mr[me] = ms[lax.div(me * owned, bs)]
    load_n.wait()

    def spread(turn):
        for p in range(n):
            afull[p * owned:(p + 1) * owned] = al[turn, p].astype(jnp.float32)

    step_columns = min(1024, bs * bs)

    def accumulate(s, carry, fresh=False):
        if fresh:
            rows_b, rows_c = piece(bg, coords[1, 0, s]), piece(cfull, coords[2, 0, s])
        block_a = piece(afull, coords[0, 0, s]).astype(jnp.bfloat16)
        part = jnp.zeros((bs, rank), jnp.float32)
        for first in range(0, bs * bs, step_columns):
            if fresh:
                rows = jnp.concatenate(
                    [
                        (rows_b[j:j + 1] * rows_c).astype(jnp.bfloat16)
                        for j in range(first // bs, (first + step_columns) // bs)
                    ]
                )
                panel[s, first:first + step_columns] = rows
            else:
                rows = panel[s, first:first + step_columns]
            model = lax.dot_general(
                block_a, rows, (((1,), (1,)), ((), ())), preferred_element_type=jnp.float32
            )
            here = cnt[s, :, first:first + step_columns].astype(jnp.float32)
            ratio = (here / model).astype(jnp.bfloat16)
            part += jnp.dot(ratio, rows, preferred_element_type=jnp.float32)
        part = part * live_weight(s)
        for q in range(RB1):
            phi[q * bs:(q + 1) * bs] += jnp.where(is_block(coords[0, 0, s], q), part, 0.0)
        return carry

    def scattered(turn):
        for p in range(n):
            ps[p] = phi[p * owned:(p + 1) * owned]
        loop(n, lambda d: phi_copy(turn, d, me).start())
        pr[turn, me] = ps[me]
        loop(n, lambda d: phi_copy(turn, d, source(d)).wait_recv())
        total = pr[turn, 0]
        for p in range(1, n):
            total += pr[turn, p]
        return total

    for e in range(n_ja):
        loop(n_ka, lambda d: a_along(e, d, lax.rem(ka + n_ka - d, n_ka)).wait_recv())
    spread(0)
    loop(n, lambda d: mass_copy(d, me).start())
    lax.fori_loop(0, slots, functools.partial(accumulate, fresh=True), 0, unroll=True)
    total = scattered(0)
    loop(n, lambda d: mass_copy(d, source(d)).wait_recv())
    mass = mr[0]
    for p in range(1, n):
        mass += mr[p]
    updated = aown[...] * total / mass
    alow[1] = updated.astype(jnp.bfloat16)
    loop(n, lambda d: a_copy(d, me).start())
    phi[...] = jnp.zeros_like(phi)
    loop(n, lambda d: phi_copy(0, d, me).wait_send())
    aown[...] = updated
    al[1, me] = alow[1]
    loop(n, lambda d: a_copy(d, source(d)).wait_recv())
    spread(1)
    lax.fori_loop(0, slots, accumulate, 0, unroll=True)
    total = scattered(1)
    out[...] = aown[...] * total / mass

    loop(n_ka, lambda d: b_copy(d, ka).wait_send())
    loop(n_ia, lambda d: c_copy(d, ia).wait_send())
    if halves == 2:
        loop(n_ka, lambda d: b_hand(d, part).wait_send())
    loop(n_ja, lambda d: a_across(d, ja).wait_send())
    for e in range(n_ja):
        loop(n_ka, lambda d: a_along(e, d, ka).wait_send())
    loop(n, lambda d: a_copy(d, me).wait_send())
    loop(n, lambda d: mass_copy(d, me).wait_send())
    loop(n, lambda d: phi_copy(1, d, me).wait_send())


def local(n_ia, n_ja, n_ka, block_coords, live_blocks, counts, factor_a, factor_b, factor_c):
    slots = block_coords.shape[-2]
    bs, cells = counts.shape[-2:]
    owned, rank = factor_a.shape
    rb = factor_b.shape[0]
    rc, wc = factor_c.shape
    n = n_ja * n_ka
    f32, bf16 = jnp.float32, jnp.bfloat16
    smem = pl.BlockSpec(memory_space=pltpu.SMEM)
    hbm = pl.BlockSpec(memory_space=pl.ANY)
    dma = pltpu.SemaphoreType.DMA
    return pl.pallas_call(
        functools.partial(kernel, n_ia, n_ja, n_ka, bs),
        out_shape=jax.ShapeDtypeStruct((owned, rank), f32),
        in_specs=[smem, smem, hbm, hbm, hbm, hbm],
        out_specs=pl.BlockSpec(memory_space=pltpu.VMEM),
        scratch_shapes=[
            pltpu.VMEM((slots, bs, cells), jnp.int32),
            pltpu.VMEM((n_ka * rb, rank), f32),
            pltpu.VMEM((n_ia * wc, rc), f32),
            pltpu.VMEM((rc, rank), f32),
            pltpu.VMEM((owned, rank), f32),
            pltpu.VMEM((2, owned, rank), bf16),
            pltpu.VMEM((2, n, owned, rank), bf16),
            pltpu.VMEM((RB1 * bs, rank), f32),
            pltpu.VMEM((slots, cells, rank), bf16),
            pltpu.VMEM((RB1 * bs, rank), f32),
            pltpu.VMEM((n, owned, rank), f32),
            pltpu.VMEM((2, n, owned, rank), f32),
            pltpu.VMEM((RB1, 1, rank), f32),
            pltpu.VMEM((n, 1, rank), f32),
            dma((4,)),
            dma((2, n_ka)),
            dma((2, n_ka)),
            dma((n_ia,)),
            dma((n_ia,)),
            dma((5, n)),
            dma((5, n)),
        ],
        compiler_params=pltpu.CompilerParams(
            collective_id=0, has_side_effects=True, vmem_limit_bytes=56 * 1024 * 1024
        ),
    )(
        jnp.swapaxes(block_coords, 3, 4).reshape(3, 1, slots), live_blocks.reshape(1),
        counts.reshape(slots, bs, cells), factor_a, factor_b, factor_c.T,
    )


def solution(mesh):
    placed = (
        P("ia", "ja", "ka", None, None),
        P("ia", "ja", "ka"),
        P("ia", "ja", "ka", None, None, None),
        P(("ia", "ja", "ka"), None),
        P(("ja", "ka"), None),
        P("ka", "ia"),
    )
    body = functools.partial(local, mesh.shape["ia"], mesh.shape["ja"], mesh.shape["ka"])
    return jax.shard_map(
        body, mesh=mesh, in_specs=placed, out_specs=P(("ia", "ja", "ka"), None), check_vma=False
    )
```

```python
import functools

import jax
import jax.numpy as jnp
from jax import lax
from jax.experimental import pallas as pl
from jax.experimental.pallas import tpu as pltpu
from jax.sharding import PartitionSpec as P

RB1 = 4
RB2 = 4
RB3 = 4
MESH = pl.DeviceIdType.MESH


def loop(count, body, order=None):
    if count <= 8:
        for d in order or range(1, count):
            body(d)
    else:

        def step(d, carry):
            body(d)
            return carry

        lax.fori_loop(1, count, step, 0)


def kernel(
    n_ia, n_ja, n_ka, bs,
    coords_in, live_in, counts, fa, fb, fc, out, coords, live,
    cnt, bg, cg, cfull, aown, alow, al, afull, panel, phi, ps, pr, ms, mr,
    local_sem, b_send, b_recv, c_send, c_recv, g_send, g_recv,
):
    n = n_ja * n_ka
    ia, ja, ka = lax.axis_index("ia"), lax.axis_index("ja"), lax.axis_index("ka")
    me = ja * n_ka + ka
    slots = cnt.shape[0]
    owned, rank = aown.shape
    rb = fb.shape[0]
    wc = fc.shape[0]

    far_first = sorted(range(1, n), key=lambda d: -min(d % n_ka, n_ka - d % n_ka))

    def group(d):
        t = lax.rem(me + d, n)
        return {"ja": lax.div(t, n_ka), "ka": lax.rem(t, n_ka)}

    def source(d):
        return lax.rem(me + n - d, n)

    load_a = pltpu.make_async_copy(fa, aown, local_sem.at[0])
    own_rows = pl.ds(pl.multiple_of(ka * rb, rb), rb)
    load_b = pltpu.make_async_copy(fb, bg.at[own_rows], local_sem.at[1])
    own_ranks = pl.ds(pl.multiple_of(ia * wc, wc), wc)
    load_c = pltpu.make_async_copy(fc, cg.at[own_ranks], local_sem.at[2])
    load_n = pltpu.make_async_copy(counts, cnt, local_sem.at[3])
    load_a.start()
    load_b.start()
    load_c.start()
    load_n.start()
    load_where = pltpu.make_async_copy(coords_in, coords, local_sem.at[4])
    load_live = pltpu.make_async_copy(live_in, live, local_sem.at[5])
    load_where.start()
    load_live.start()

    barrier = pltpu.get_barrier_semaphore()
    for axis, here, count in (("ka", ka, n_ka), ("ja", ja, n_ja), ("ia", ia, n_ia)):
        loop(
            count,
            lambda d: pl.semaphore_signal(
                barrier, inc=1, device_id={axis: lax.rem(here + d, count)}, device_id_type=MESH
            ),
        )
    load_a.wait()
    alow[0] = aown[...].astype(jnp.bfloat16)
    pl.semaphore_wait(barrier, n_ka + n_ja + n_ia - 3)

    halves = 2 if n_ia % 2 == 0 and rb % 16 == 0 else 1
    hb = rb // halves
    part = lax.rem(ia, halves)
    partner = ia + 1 - 2 * part

    def b_rows(whose, half):
        return bg.at[pl.ds(pl.multiple_of(whose * rb + half * hb, hb), hb)]

    def b_copy(d, whose):
        return pltpu.make_async_remote_copy(
            src_ref=fb.at[pl.ds(pl.multiple_of(part * hb, hb), hb)], dst_ref=b_rows(whose, part),
            send_sem=b_send.at[0, d], recv_sem=b_recv.at[0, d],
            device_id={"ka": lax.rem(ka + d, n_ka)}, device_id_type=MESH,
        )

    def b_hand(d, half):
        rows = b_rows(lax.rem(ka + n_ka - d, n_ka), half)
        return pltpu.make_async_remote_copy(
            src_ref=rows, dst_ref=rows, send_sem=b_send.at[1, d], recv_sem=b_recv.at[1, d],
            device_id={"ia": partner}, device_id_type=MESH,
        )

    def c_copy(d, whose):
        ranks = pl.ds(pl.multiple_of(whose * wc, wc), wc)
        return pltpu.make_async_remote_copy(
            src_ref=fc, dst_ref=cg.at[ranks], send_sem=c_send.at[d], recv_sem=c_recv.at[d],
            device_id={"ia": lax.rem(ia + d, n_ia)}, device_id_type=MESH,
        )

    def a_copy(d, whose):
        return pltpu.make_async_remote_copy(
            src_ref=alow.at[1], dst_ref=al.at[1, whose],
            send_sem=g_send.at[1, d], recv_sem=g_recv.at[1, d],
            device_id=group(d), device_id_type=MESH,
        )

    def a_across(d, whose):
        return pltpu.make_async_remote_copy(
            src_ref=alow.at[0], dst_ref=al.at[0, whose * n_ka + ka],
            send_sem=g_send.at[0, d * n_ka], recv_sem=g_recv.at[0, d * n_ka],
            device_id={"ja": lax.rem(ja + d, n_ja)}, device_id_type=MESH,
        )

    def a_along(e, d, whose):
        other = lax.rem(ja + n_ja - e, n_ja) * n_ka
        return pltpu.make_async_remote_copy(
            src_ref=alow.at[0] if isinstance(e, int) and e == 0 else al.at[0, other + ka],
            dst_ref=al.at[0, other + whose],
            send_sem=g_send.at[0, e * n_ka + d], recv_sem=g_recv.at[0, e * n_ka + d],
            device_id={"ka": lax.rem(ka + d, n_ka)}, device_id_type=MESH,
        )

    def phi_copy(turn, d, whose):
        return pltpu.make_async_remote_copy(
            src_ref=ps.at[lax.rem(me + d, n)], dst_ref=pr.at[turn, whose],
            send_sem=g_send.at[2 + turn, d], recv_sem=g_recv.at[2 + turn, d],
            device_id=group(d), device_id_type=MESH,
        )

    def mass_copy(d, whose):
        block = lax.div(lax.rem(me + d, n) * owned, bs)
        return pltpu.make_async_remote_copy(
            src_ref=ms.at[block], dst_ref=mr.at[whose],
            send_sem=g_send.at[4, d], recv_sem=g_recv.at[4, d],
            device_id=group(d), device_id_type=MESH,
        )

    loop(n_ka, lambda d: b_copy(d, ka).start())
    loop(n_ia, lambda d: c_copy(d, ia).start())
    loop(n_ja, lambda d: a_across(d, ja).start())
    loop(n_ka, lambda d: a_along(0, d, ka).start())
    al[0, me] = alow[0]

    phi[...] = jnp.zeros_like(phi)
    ms[...] = jnp.zeros_like(ms)
    load_where.wait()
    load_live.wait()
    load_b.wait()
    load_c.wait()


    def across(e):
        a_across(e, lax.rem(ja + n_ja - e, n_ja)).wait_recv()
        loop(n_ka, lambda d: a_along(e, d, ka).start())

    loop(n_ja, across)

    def hand_on(d):
        b_copy(d, lax.rem(ka + n_ka - d, n_ka)).wait_recv()
        if halves == 2:
            b_hand(d, part).start()

    loop(n_ka, hand_on)
    loop(n_ia, lambda d: c_copy(d, lax.rem(ia + n_ia - d, n_ia)).wait_recv())
    cfull[...] = cg[...].T
    if halves == 2:
        loop(n_ka, lambda d: b_hand(d, 1 - part).wait_recv())

    def is_block(index, q):
        return jnp.full((bs, rank), index, jnp.int32) == q

    def live_weight(s):
        return jnp.minimum(jnp.maximum(live[0] - s, 0), 1).astype(jnp.float32)

    def piece(ref, index):
        found = ref[:bs]
        for q in range(1, ref.shape[0] // bs):
            found = jnp.where(is_block(index, q), ref[q * bs:(q + 1) * bs], found)
        return found

    def build(s, carry):
        rows_b = piece(bg, coords[1, 0, s])
        rows_c = piece(cfull, coords[2, 0, s])
        mass = jnp.sum(rows_b, axis=0, keepdims=True) * jnp.sum(rows_c, axis=0, keepdims=True)
        mass = mass * live_weight(s)
        for q in range(RB1):
            ms[q] += jnp.where(is_block(coords[0, 0, s], q)[:1], mass, 0.0)
        return carry

    lax.fori_loop(0, slots, build, 0)
    mr[me] = ms[lax.div(me * owned, bs)]
    load_n.wait()

    def spread(turn):
        for p in range(n):
            afull[p * owned:(p + 1) * owned] = al[turn, p].astype(jnp.float32)

    step_columns = min(1024, bs * bs)

    steps = [(s, first) for s in range(slots) for first in range(0, bs * bs, step_columns)]

    def accumulate(fresh):
        def model_of(item, block_a, rows_b, rows_c):
            s, first = item
            if fresh:
                rows = jnp.concatenate(
                    [
                        (rows_b[j:j + 1] * rows_c).astype(jnp.bfloat16)
                        for j in range(first // bs, (first + step_columns) // bs)
                    ]
                )
                panel[s, first:first + step_columns] = rows
            else:
                rows = panel[s, first:first + step_columns]
            model = lax.dot_general(
                block_a, rows, (((1,), (1,)), ((), ())), preferred_element_type=jnp.float32
            )
            return rows, model

        def start(item):
            s, first = item
            if first == 0:
                block_a = piece(afull, coords[0, 0, s]).astype(jnp.bfloat16)
                held[:] = [block_a, None, None]
                if fresh:
                    held[1:] = [piece(bg, coords[1, 0, s]), piece(cfull, coords[2, 0, s])]
            return model_of(item, *held)

        held = []
        part = None
        ahead = start(steps[0])
        for at, (s, first) in enumerate(steps):
            rows, model = ahead
            if at + 1 < len(steps):
                ahead = start(steps[at + 1])
            here = cnt[s, :, first:first + step_columns].astype(jnp.float32)
            ratio = (here / model).astype(jnp.bfloat16)
            term = jnp.dot(ratio, rows, preferred_element_type=jnp.float32)
            part = term if first == 0 else part + term
            if first + step_columns == bs * bs:
                part = part * live_weight(s)
                for q in range(RB1):
                    phi[q * bs:(q + 1) * bs] += jnp.where(is_block(coords[0, 0, s], q), part, 0.0)

    def scattered(turn):
        for p in range(n):
            ps[p] = phi[p * owned:(p + 1) * owned]
        loop(n, lambda d: phi_copy(turn, d, me).start(), far_first)
        pr[turn, me] = ps[me]
        loop(n, lambda d: phi_copy(turn, d, source(d)).wait_recv())
        total = pr[turn, 0]
        for p in range(1, n):
            total += pr[turn, p]
        return total

    for e in range(n_ja):
        loop(n_ka, lambda d: a_along(e, d, lax.rem(ka + n_ka - d, n_ka)).wait_recv())
    spread(0)
    loop(n, lambda d: mass_copy(d, me).start())
    accumulate(True)
    total = scattered(0)
    loop(n, lambda d: mass_copy(d, source(d)).wait_recv())
    mass = mr[0]
    for p in range(1, n):
        mass += mr[p]
    updated = aown[...] * total / mass
    alow[1] = updated.astype(jnp.bfloat16)
    loop(n, lambda d: a_copy(d, me).start(), far_first)
    phi[...] = jnp.zeros_like(phi)
    loop(n, lambda d: phi_copy(0, d, me).wait_send())
    aown[...] = updated
    al[1, me] = alow[1]
    loop(n, lambda d: a_copy(d, source(d)).wait_recv())
    spread(1)
    accumulate(False)
    total = scattered(1)
    out[...] = aown[...] * total / mass

    loop(n_ka, lambda d: b_copy(d, ka).wait_send())
    loop(n_ia, lambda d: c_copy(d, ia).wait_send())
    if halves == 2:
        loop(n_ka, lambda d: b_hand(d, part).wait_send())
    loop(n_ja, lambda d: a_across(d, ja).wait_send())
    for e in range(n_ja):
        loop(n_ka, lambda d: a_along(e, d, ka).wait_send())
    loop(n, lambda d: a_copy(d, me).wait_send())
    loop(n, lambda d: mass_copy(d, me).wait_send())
    loop(n, lambda d: phi_copy(1, d, me).wait_send())


def local(n_ia, n_ja, n_ka, block_coords, live_blocks, counts, factor_a, factor_b, factor_c):
    slots = block_coords.shape[-2]
    bs, cells = counts.shape[-2:]
    owned, rank = factor_a.shape
    rb = factor_b.shape[0]
    rc, wc = factor_c.shape
    n = n_ja * n_ka
    f32, bf16 = jnp.float32, jnp.bfloat16
    hbm = pl.BlockSpec(memory_space=pl.ANY)
    dma = pltpu.SemaphoreType.DMA
    return pl.pallas_call(
        functools.partial(kernel, n_ia, n_ja, n_ka, bs),
        out_shape=jax.ShapeDtypeStruct((owned, rank), f32),
        in_specs=[hbm] * 6,
        out_specs=pl.BlockSpec(memory_space=pltpu.VMEM),
        scratch_shapes=[
            pltpu.SMEM((3, 1, slots), jnp.int32),
            pltpu.SMEM((1,), jnp.int32),
            pltpu.VMEM((slots, bs, cells), jnp.int32),
            pltpu.VMEM((n_ka * rb, rank), f32),
            pltpu.VMEM((n_ia * wc, rc), f32),
            pltpu.VMEM((rc, rank), f32),
            pltpu.VMEM((owned, rank), f32),
            pltpu.VMEM((2, owned, rank), bf16),
            pltpu.VMEM((2, n, owned, rank), bf16),
            pltpu.VMEM((RB1 * bs, rank), f32),
            pltpu.VMEM((slots, cells, rank), bf16),
            pltpu.VMEM((RB1 * bs, rank), f32),
            pltpu.VMEM((n, owned, rank), f32),
            pltpu.VMEM((2, n, owned, rank), f32),
            pltpu.VMEM((RB1, 1, rank), f32),
            pltpu.VMEM((n, 1, rank), f32),
            dma((6,)),
            dma((2, n_ka)),
            dma((2, n_ka)),
            dma((n_ia,)),
            dma((n_ia,)),
            dma((5, n)),
            dma((5, n)),
        ],
        compiler_params=pltpu.CompilerParams(
            collective_id=0, has_side_effects=True, vmem_limit_bytes=56 * 1024 * 1024
        ),
    )(
        jnp.swapaxes(block_coords, 3, 4).reshape(3, 1, slots), live_blocks.reshape(1),
        counts.reshape(slots, bs, cells), factor_a, factor_b, factor_c.T,
    )


def solution(mesh):
    placed = (
        P("ia", "ja", "ka", None, None),
        P("ia", "ja", "ka"),
        P("ia", "ja", "ka", None, None, None),
        P(("ia", "ja", "ka"), None),
        P(("ja", "ka"), None),
        P("ka", "ia"),
    )
    body = functools.partial(local, mesh.shape["ia"], mesh.shape["ja"], mesh.shape["ka"])
    return jax.shard_map(
        body, mesh=mesh, in_specs=placed, out_specs=P(("ia", "ja", "ka"), None), check_vma=False
    )
```
